256 devices in a mesh: pipe: 16 (over z, core), dp: 4 (over x), tensor: 4 (over y).
Axes of the slice: x: 4, y: 4, z: 8, core: 2. Of those that a mesh axis runs over, the one named last changes fastest.
Arguments:
- acts: bfloat16 [16, 2048, 8192], P('pipe', 'dp', 'tensor'), may hold values from -6 to 6
- grads: bfloat16 [16, 2048, 8192], P('pipe', 'dp', 'tensor'), may hold values from -6 to 6
- sketch_index: int32 [16, 2, 16], P('pipe'), may hold values from 0 to 63, as said below
- sketch_values: bfloat16 [16, 2, 16, 128, 32], P('pipe'), may hold values from -0.125 to 0.125
Outputs:
- basis: float32 [16384, 256], P(('pipe', 'tensor'), 'dp')
The draws below stay inside these ranges and needn't reach their ends.
Inputs may be any that keep to these rules, and one draw needn't show every extreme that they name: `sketch_index`: the 16 blocks of each sketch are distinct.
All inputs are finite; a program needn't handle non-finite values.
Results may differ from the reference program's by a relative error of at most 0.0003.
Values sent between devices are 32-bit elements; how exact they have to be, the bound alone decides.
A program may use at most 64 MiB of HBM per device.

```python
import jax
import jax.numpy as jnp
from jax import lax

D = 8192
NSEL = 16
SKETCH = 32
RANK = 256
ITERS = 2
E_DEV = 128
TOK_EX = 4
SECTIONS = 16
TOKENS = 2048
EXAMPLES = 512
K_TOTAL = 16384
N_DP = 4


def draw_sketch_index(key, part):
    keys = jax.random.split(jax.random.fold_in(key, 7), SECTIONS * 2)

    def pick(single):
        return jax.random.permutation(single, D // 128)[:NSEL]
    rows = jax.vmap(pick)(keys)
    return rows.reshape(SECTIONS, 2, NSEL).astype(jnp.int32)


def block_levels(rng, dims, shards, least, high):
    gain = 1.0
    for axis_at, parts in shards:
        draws = jax.random.uniform(jax.random.fold_in(jax.random.fold_in(rng, 6), axis_at), (parts,), jnp.float32, least / len(shards), high / len(shards))
        gain = gain * jnp.repeat(jnp.exp(draws), dims[axis_at] // parts).reshape((-1,) + (1,) * (len(dims) - 1 - axis_at))
    return gain


def bell_draw(own_key, shape, deviation, bound, cuts=(), kind=jnp.bfloat16):
    drawn = deviation * jax.random.normal(own_key, shape, jnp.float32)
    if cuts:
        drawn = drawn * block_levels(own_key, shape, cuts, -0.22, 0.18)
    return jnp.clip(drawn, -bound, bound).astype(kind)


def setup_inputs(seed: int = 0) -> dict:
    splits = jax.random.split(jax.random.key(seed), 5)
    acts = bell_draw(splits[0], (SECTIONS, TOKENS, D), 1.0, 6.0, ((0, 16), (1, 4), (2, 4)))
    grads = bell_draw(splits[1], (SECTIONS, TOKENS, D), 1.0, 6.0, ((0, 16), (1, 4), (2, 4)))
    sketch_index = draw_sketch_index(jax.random.fold_in(splits[4], 71), 0)
    sketch_values = bell_draw(splits[3], (SECTIONS, 2, NSEL, 128, SKETCH), (NSEL * 128) ** -0.5, 0.125, ((0, 16),))
    return {"acts": acts, "grads": grads, "sketch_index": sketch_index, "sketch_values": sketch_values}


def mm(a, b):
    return jnp.matmul(a, b, precision=lax.Precision.HIGHEST)

def orthonormal(block):
    lower = jnp.linalg.cholesky(mm(block.T, block))
    return lax.linalg.triangular_solve(lower, block, left_side=False, lower=True, transpose_a=True)

def merge_pair(first, second):
    joined = jnp.concatenate([first, second], axis=1)
    if joined.shape[1] <= RANK:
        return joined
    q_basis = orthonormal(joined[:, :RANK] + joined[:, RANK:])
    for turn in range(ITERS):
        q_basis = orthonormal(mm(joined, mm(joined.T, q_basis)))
    weights = mm(joined.T, q_basis)
    lower = jnp.linalg.cholesky(mm(weights.T, weights))
    return mm(q_basis, lower)

def build_sketch(index_row, values_row, blocks):
    onehot = (index_row[:, None] == jnp.arange(blocks, dtype=jnp.int32)[None, :]).astype(jnp.float32)
    dense = jnp.einsum('ij,icd->jcd', onehot, values_row.astype(jnp.float32))
    return dense.reshape(blocks * 128, SKETCH).astype(jnp.bfloat16)

def section_sketch(items):
    acts_s, grads_s, index_s, values_s = items
    blocks = acts_s.shape[1] // 128
    sketch_in = build_sketch(index_s[0], values_s[0], blocks)
    sketch_out = build_sketch(index_s[1], values_s[1], blocks)
    left = jnp.dot(acts_s.astype(jnp.float32), sketch_in.astype(jnp.float32), preferred_element_type=jnp.float32).reshape(-1, TOK_EX, SKETCH)
    right = jnp.dot(grads_s.astype(jnp.float32), sketch_out.astype(jnp.float32), preferred_element_type=jnp.float32).reshape(-1, TOK_EX, SKETCH)
    outer = jnp.einsum('etk,etl->ekl', left, right, precision=lax.Precision.HIGHEST)
    return outer.reshape(outer.shape[0], SKETCH * SKETCH)

def reference(acts, grads, sketch_index, sketch_values):
    per_section = lax.map(section_sketch, (acts, grads, sketch_index, sketch_values))
    sketched = jnp.transpose(per_section, (1, 0, 2)).reshape(EXAMPLES, K_TOTAL)
    bases = [sketched[d * E_DEV:(d + 1) * E_DEV].T for d in range(N_DP)]
    while len(bases) > 1:
        bases = [merge_pair(bases[2 * k], bases[2 * k + 1]) for k in range(len(bases) // 2)]
    return bases[0]
```

```python
import jax
import jax.numpy as jnp
from jax import lax
from jax.sharding import PartitionSpec as P

RANK = 256
ITERS = 2
TOK_EX = 4


def mm(a, b):
    return jnp.matmul(a, b, precision=lax.Precision.HIGHEST)


def mm_tn(a, b):
    return lax.dot_general(a, b, (((0,), (0,)), ((), ())), precision=lax.Precision.HIGHEST)


def solve_lower_t(lower, block):
    return lax.linalg.triangular_solve(lower, block, left_side=False, lower=True, transpose_a=True)


def merged_coords(gram):
    cols = gram.shape[0]
    eye = jnp.eye(RANK, dtype=gram.dtype)
    pick = jnp.concatenate([eye] * (cols // RANK), axis=0)
    lower = jnp.linalg.cholesky(mm_tn(pick, mm(gram, pick)))
    coords = solve_lower_t(lower, pick)
    for turn in range(ITERS):
        image = mm(gram, coords)
        lower = jnp.linalg.cholesky(mm_tn(image, mm(gram, image)))
        coords = solve_lower_t(lower, image)
    weights = mm(gram, coords)
    lower = jnp.linalg.cholesky(mm_tn(weights, weights))
    return mm(coords, lower)


def shards(acts, grads, sketch_index, sketch_values):
    local_width = acts.shape[2]
    blocks = local_width // 128
    width = sketch_values.shape[4]
    tensor_pos = lax.axis_index("tensor")
    tensor_count = lax.axis_size("tensor")
    dp_pos = lax.axis_index("dp")
    dp_count = lax.axis_size("dp")
    span = jnp.arange(blocks, dtype=jnp.int32) + tensor_pos * blocks
    onehot = (sketch_index[0][:, :, None] == span[None, None, :]).astype(jnp.bfloat16)
    local = jnp.einsum(
        "sij,sicd->sjcd", onehot, sketch_values[0], preferred_element_type=jnp.float32
    )
    local = local.astype(jnp.bfloat16).reshape(2, local_width, width)
    left_part = jnp.dot(acts[0], local[0], preferred_element_type=jnp.float32)
    right_part = jnp.dot(grads[0], local[1], preferred_element_type=jnp.float32)
    both = lax.psum(jnp.concatenate([left_part, right_part], axis=1), "tensor")
    both = lax.all_gather(both, "dp", axis=0, tiled=True)
    left_all = both[:, :width].reshape(-1, TOK_EX, width)
    right_all = both[:, width:].reshape(-1, TOK_EX, width)
    outer = jnp.einsum("etk,etl->ekl", left_all, right_all, precision=lax.Precision.HIGHEST)
    joined_t = outer.reshape(outer.shape[0], -1)
    gram = lax.psum(mm(joined_t, joined_t.T), "pipe")
    coords = merged_coords(gram)
    part_rows = joined_t.shape[1] // tensor_count
    rows = lax.dynamic_slice_in_dim(joined_t, tensor_pos * part_rows, part_rows, 1)
    own_columns = coords.shape[1] // dp_count
    coords = lax.dynamic_slice_in_dim(coords, dp_pos * own_columns, own_columns, 1)
    return mm_tn(rows, coords)


def solution(mesh):
    placed = (
        P("pipe", "dp", "tensor"),
        P("pipe", "dp", "tensor"),
        P("pipe", None, None),
        P("pipe", None, None, None, None),
    )
    return jax.shard_map(
        shards, mesh=mesh, in_specs=placed, out_specs=P(("pipe", "tensor"), "dp"), check_vma=False
    )
```

```python
import jax
import jax.numpy as jnp
from jax import lax
from jax.sharding import PartitionSpec as P

RANK = 256
ITERS = 2
TOK_EX = 4


def mm(a, b):
    return jnp.matmul(a, b, precision=lax.Precision.HIGHEST)


def mm_tn(a, b):
    return lax.dot_general(a, b, (((0,), (0,)), ((), ())), precision=lax.Precision.HIGHEST)


def exchange(block, axis, bit):
    count = lax.axis_size(axis)
    return lax.ppermute(block, axis, [(i, i ^ (1 << bit)) for i in range(count)])


def butterfly_sum(block, axis):
    for bit in range(lax.axis_size(axis).bit_length() - 1):
        block = block + exchange(block, axis, bit)
    return block


def halving_doubling_sum(block, axis):
    position = lax.axis_index(axis)
    bits = lax.axis_size(axis).bit_length() - 1
    for bit in range(bits):
        half = block.shape[0] // 2
        upper = jnp.right_shift(position, bit) % 2 == 1
        keep = jnp.where(upper, block[half:], block[:half])
        give = jnp.where(upper, block[:half], block[half:])
        block = keep + exchange(give, axis, bit)
    return doubling_gather(block, axis, reversed(range(bits)))


def doubling_gather(block, axis, bits):
    position = lax.axis_index(axis)
    for bit in bits:
        upper = jnp.right_shift(position, bit) % 2 == 1
        other = exchange(block, axis, bit)
        block = jnp.where(
            upper, jnp.concatenate([other, block], 0), jnp.concatenate([block, other], 0)
        )
    return block


def solve_lower_t(lower, block):
    return lax.linalg.triangular_solve(lower, block, left_side=False, lower=True, transpose_a=True)


def merged_coords(gram):
    cols = gram.shape[0]
    eye = jnp.eye(RANK, dtype=gram.dtype)
    pick = jnp.concatenate([eye] * (cols // RANK), axis=0)
    lower = jnp.linalg.cholesky(mm_tn(pick, mm(gram, pick)))
    coords = solve_lower_t(lower, pick)
    for turn in range(ITERS):
        image = mm(gram, coords)
        lower = jnp.linalg.cholesky(mm_tn(image, mm(gram, image)))
        coords = solve_lower_t(lower, image)
    weights = mm(gram, coords)
    lower = jnp.linalg.cholesky(mm_tn(weights, weights))
    return mm(coords, lower)


def shards(acts, grads, sketch_index, sketch_values):
    local_width = acts.shape[2]
    blocks = local_width // 128
    width = sketch_values.shape[4]
    tensor_pos = lax.axis_index("tensor")
    tensor_count = lax.axis_size("tensor")
    dp_pos = lax.axis_index("dp")
    dp_count = lax.axis_size("dp")
    span = jnp.arange(blocks, dtype=jnp.int32) + tensor_pos * blocks
    onehot = (sketch_index[0][:, :, None] == span[None, None, :]).astype(jnp.bfloat16)
    local = jnp.einsum(
        "sij,sicd->sjcd", onehot, sketch_values[0], preferred_element_type=jnp.float32
    )
    local = local.astype(jnp.bfloat16).reshape(2, local_width, width)
    left_part = jnp.dot(acts[0], local[0], preferred_element_type=jnp.float32)
    right_part = jnp.dot(grads[0], local[1], preferred_element_type=jnp.float32)
    both = butterfly_sum(jnp.concatenate([left_part, right_part], axis=1), "tensor")
    dp_bits = dp_count.bit_length() - 1
    both = doubling_gather(both, "dp", range(dp_bits))
    left_all = both[:, :width].reshape(-1, TOK_EX, width)
    right_all = both[:, width:].reshape(-1, TOK_EX, width)
    outer = jnp.einsum("etk,etl->ekl", left_all, right_all, precision=lax.Precision.HIGHEST)
    joined_t = outer.reshape(outer.shape[0], -1)
    gram = halving_doubling_sum(mm(joined_t, joined_t.T), "pipe")
    coords = merged_coords(gram)
    part_rows = joined_t.shape[1] // tensor_count
    rows = lax.dynamic_slice_in_dim(joined_t, tensor_pos * part_rows, part_rows, 1)
    own_columns = coords.shape[1] // dp_count
    coords = lax.dynamic_slice_in_dim(coords, dp_pos * own_columns, own_columns, 1)
    return mm_tn(rows, coords)


def solution(mesh):
    placed = (
        P("pipe", "dp", "tensor"),
        P("pipe", "dp", "tensor"),
        P("pipe", None, None),
        P("pipe", None, None, None, None),
    )
    return jax.shard_map(
        shards, mesh=mesh, in_specs=placed, out_specs=P(("pipe", "tensor"), "dp"), check_vma=False
    )
```

```python
import jax
import jax.numpy as jnp
from jax import lax
from jax.sharding import PartitionSpec as P

RANK = 256
ITERS = 2
TOK_EX = 4


def mm(a, b):
    return jnp.matmul(a, b, precision=lax.Precision.HIGHEST)


def mm_tn(a, b):
    return lax.dot_general(a, b, (((0,), (0,)), ((), ())), precision=lax.Precision.HIGHEST)


def exchange(block, axis, bit):
    count = lax.axis_size(axis)
    return lax.ppermute(block, axis, [(i, i ^ (1 << bit)) for i in range(count)])


def butterfly_sum(block, axis):
    for bit in range(lax.axis_size(axis).bit_length() - 1):
        block = block + exchange(block, axis, bit)
    return block


def halving_doubling_sum(block, axis):
    position = lax.axis_index(axis)
    bits = lax.axis_size(axis).bit_length() - 1
    for bit in range(bits):
        half = block.shape[0] // 2
        upper = jnp.right_shift(position, bit) % 2 == 1
        keep = jnp.where(upper, block[half:], block[:half])
        give = jnp.where(upper, block[:half], block[half:])
        block = keep + exchange(give, axis, bit)
    return doubling_gather(block, axis, reversed(range(bits)))


def doubling_gather(block, axis, bits):
    position = lax.axis_index(axis)
    for bit in bits:
        upper = jnp.right_shift(position, bit) % 2 == 1
        other = exchange(block, axis, bit)
        block = jnp.where(
            upper, jnp.concatenate([other, block], 0), jnp.concatenate([block, other], 0)
        )
    return block


def solve_lower_t(lower, block):
    return lax.linalg.triangular_solve(lower, block, left_side=False, lower=True, transpose_a=True)


def merged_coords(gram):
    cols = gram.shape[0]
    eye = jnp.eye(RANK, dtype=gram.dtype)
    pick = jnp.concatenate([eye] * (cols // RANK), axis=0)
    norms = jnp.sqrt(jnp.sum(pick * mm(gram, pick), axis=0))
    coords = pick / norms[None, :]
    for turn in range(ITERS):
        image = mm(gram, coords)
        lower = jnp.linalg.cholesky(mm_tn(image, mm(gram, image)))
        coords = solve_lower_t(lower, image)
    weights = mm(gram, coords)
    lower = jnp.linalg.cholesky(mm_tn(weights, weights))
    return mm(coords, lower)


def shards(acts, grads, sketch_index, sketch_values):
    local_width = acts.shape[2]
    blocks = local_width // 128
    width = sketch_values.shape[4]
    tensor_pos = lax.axis_index("tensor")
    tensor_count = lax.axis_size("tensor")
    dp_pos = lax.axis_index("dp")
    dp_count = lax.axis_size("dp")
    span = jnp.arange(blocks, dtype=jnp.int32) + tensor_pos * blocks
    onehot = (sketch_index[0][:, :, None] == span[None, None, :]).astype(jnp.bfloat16)
    local = jnp.einsum(
        "sij,sicd->sjcd", onehot, sketch_values[0], preferred_element_type=jnp.float32
    )
    local = local.astype(jnp.bfloat16).reshape(2, local_width, width)
    left_part = jnp.dot(acts[0], local[0], preferred_element_type=jnp.float32)
    right_part = jnp.dot(grads[0], local[1], preferred_element_type=jnp.float32)
    both = butterfly_sum(jnp.concatenate([left_part, right_part], axis=1), "tensor")
    dp_bits = dp_count.bit_length() - 1
    both = doubling_gather(both, "dp", range(dp_bits))
    left_all = both[:, :width].reshape(-1, TOK_EX, width)
    right_all = both[:, width:].reshape(-1, TOK_EX, width)
    outer = jnp.einsum("etk,etl->ekl", left_all, right_all, precision=lax.Precision.HIGHEST)
    joined_t = outer.reshape(outer.shape[0], -1)
    gram = halving_doubling_sum(mm(joined_t, joined_t.T), "pipe")
    coords = merged_coords(gram)
    part_rows = joined_t.shape[1] // tensor_count
    rows = lax.dynamic_slice_in_dim(joined_t, tensor_pos * part_rows, part_rows, 1)
    own_columns = coords.shape[1] // dp_count
    coords = lax.dynamic_slice_in_dim(coords, dp_pos * own_columns, own_columns, 1)
    return mm_tn(rows, coords)


def solution(mesh):
    placed = (
        P("pipe", "dp", "tensor"),
        P("pipe", "dp", "tensor"),
        P("pipe", None, None),
        P("pipe", None, None, None, None),
    )
    return jax.shard_map(
        shards, mesh=mesh, in_specs=placed, out_specs=P(("pipe", "tensor"), "dp"), check_vma=False
    )
```

```python
import jax
import jax.numpy as jnp
from jax import lax
from jax.sharding import PartitionSpec as P

RANK = 256
ITERS = 2
TOK_EX = 4


def mm(a, b):
    return jnp.matmul(a, b, precision=lax.Precision.HIGHEST)


def mm_tn(a, b):
    return lax.dot_general(a, b, (((0,), (0,)), ((), ())), precision=lax.Precision.HIGHEST)


def exchange(block, axis, bit):
    count = lax.axis_size(axis)
    return lax.ppermute(block, axis, [(i, i ^ (1 << bit)) for i in range(count)])


def butterfly_sum(block, axis):
    for bit in range(lax.axis_size(axis).bit_length() - 1):
        block = block + exchange(block, axis, bit)
    return block


def halving_doubling_sum(block, axis):
    position = lax.axis_index(axis)
    bits = lax.axis_size(axis).bit_length() - 1
    for bit in range(bits):
        half = block.shape[0] // 2
        upper = jnp.right_shift(position, bit) % 2 == 1
        keep = jnp.where(upper, block[half:], block[:half])
        give = jnp.where(upper, block[:half], block[half:])
        block = keep + exchange(give, axis, bit)
    return doubling_gather(block, axis, reversed(range(bits)))


def doubling_gather(block, axis, bits):
    position = lax.axis_index(axis)
    for bit in bits:
        upper = jnp.right_shift(position, bit) % 2 == 1
        other = exchange(block, axis, bit)
        block = jnp.where(
            upper, jnp.concatenate([other, block], 0), jnp.concatenate([block, other], 0)
        )
    return block


def solve_lower_t(lower, block):
    return lax.linalg.triangular_solve(lower, block, left_side=False, lower=True, transpose_a=True)


def merged_coords(gram):
    cols = gram.shape[0]
    eye = jnp.eye(RANK, dtype=gram.dtype)
    pick = jnp.concatenate([eye] * (cols // RANK), axis=0)
    norms = jnp.sqrt(jnp.sum(pick * mm(gram, pick), axis=0))
    coords = pick / norms[None, :]
    for turn in range(ITERS):
        image = mm(gram, coords)
        lower = jnp.linalg.cholesky(mm_tn(image, mm(gram, image)))
        coords = solve_lower_t(lower, image)
    weights = mm(gram, coords)
    lower = jnp.linalg.cholesky(mm_tn(weights, weights))
    return mm(coords, lower)


def shards(acts, grads, sketch_index, sketch_values):
    local_width = acts.shape[2]
    blocks = local_width // 128
    width = sketch_values.shape[4]
    tensor_pos = lax.axis_index("tensor")
    tensor_count = lax.axis_size("tensor")
    dp_pos = lax.axis_index("dp")
    dp_count = lax.axis_size("dp")
    span = jnp.arange(blocks, dtype=jnp.int32) + tensor_pos * blocks
    onehot = (sketch_index[0][:, :, None] == span[None, None, :]).astype(jnp.bfloat16)
    local = jnp.einsum(
        "sij,sicd->sjcd", onehot, sketch_values[0], preferred_element_type=jnp.float32
    )
    local = local.astype(jnp.bfloat16).reshape(2, local_width, width)
    left_part = jnp.dot(acts[0], local[0], preferred_element_type=jnp.float32)
    right_part = jnp.dot(grads[0], local[1], preferred_element_type=jnp.float32)
    both = butterfly_sum(jnp.concatenate([left_part, right_part], axis=1), "tensor")
    dp_bits = dp_count.bit_length() - 1
    both = doubling_gather(both, "dp", range(dp_bits))
    left_all = both[:, :width].reshape(-1, TOK_EX, width)
    right_all = both[:, width:].reshape(-1, TOK_EX, width)
    outer = jnp.sum(left_all[:, :, :, None] * right_all[:, :, None, :], axis=1)
    joined_t = outer.reshape(outer.shape[0], -1)
    gram = halving_doubling_sum(mm(joined_t, joined_t.T), "pipe")
    coords = merged_coords(gram)
    part_rows = joined_t.shape[1] // tensor_count
    rows = lax.dynamic_slice_in_dim(joined_t, tensor_pos * part_rows, part_rows, 1)
    own_columns = coords.shape[1] // dp_count
    coords = lax.dynamic_slice_in_dim(coords, dp_pos * own_columns, own_columns, 1)
    return mm_tn(rows, coords)


def solution(mesh):
    placed = (
        P("pipe", "dp", "tensor"),
        P("pipe", "dp", "tensor"),
        P("pipe", None, None),
        P("pipe", None, None, None, None),
    )
    return jax.shard_map(
        shards, mesh=mesh, in_specs=placed, out_specs=P(("pipe", "tensor"), "dp"), check_vma=False
    )
```

```python
import jax
import jax.numpy as jnp
from jax import lax
from jax.sharding import PartitionSpec as P

RANK = 256
ITERS = 2
TOK_EX = 4


def mm(a, b):
    return jnp.matmul(a, b, precision=lax.Precision.HIGHEST)


def mm_tn(a, b):
    return lax.dot_general(a, b, (((0,), (0,)), ((), ())), precision=lax.Precision.HIGHEST)


RADIX = 4


def digit_of(position, level):
    return (position // RADIX ** level) % RADIX


def shifted(block, axis, level, step):
    count = lax.axis_size(axis)
    unit = RADIX ** level
    route = []
    for source in range(count):
        digit = (source // unit) % RADIX
        route.append((source, source + ((digit + step) % RADIX - digit) * unit))
    return lax.ppermute(block, axis, route)


def levels_of(axis):
    count = lax.axis_size(axis)
    levels = 0
    while RADIX ** levels < count:
        levels += 1
    return levels


def gather_level(block, axis, level):
    mine = digit_of(lax.axis_index(axis), level)
    rows = block.shape[0]
    out = jnp.zeros((RADIX * rows,) + block.shape[1:], block.dtype)
    out = lax.dynamic_update_slice_in_dim(out, block, mine * rows, 0)
    for step in range(1, RADIX):
        got = shifted(block, axis, level, step)
        out = lax.dynamic_update_slice_in_dim(out, got, ((mine - step) % RADIX) * rows, 0)
    return out


def group_sum(block, axis):
    for level in range(levels_of(axis)):
        parts = gather_level(block, axis, level)
        parts = parts.reshape((RADIX, block.shape[0]) + block.shape[1:])
        total = parts[0]
        for index in range(1, RADIX):
            total = total + parts[index]
        block = total
    return block


def group_gather(block, axis):
    for level in range(levels_of(axis)):
        block = gather_level(block, axis, level)
    return block


def scatter_gather_sum(block, axis):
    position = lax.axis_index(axis)
    levels = levels_of(axis)
    for level in range(levels):
        mine = digit_of(position, level)
        part = block.shape[0] // RADIX
        total = lax.dynamic_slice_in_dim(block, mine * part, part, 0)
        for step in range(1, RADIX):
            give = lax.dynamic_slice_in_dim(block, ((mine + step) % RADIX) * part, part, 0)
            total = total + shifted(give, axis, level, step)
        block = total
    for level in reversed(range(levels)):
        block = gather_level(block, axis, level)
    return block


def solve_lower_t(lower, block):
    return lax.linalg.triangular_solve(lower, block, left_side=False, lower=True, transpose_a=True)


def merged_coords(gram):
    cols = gram.shape[0]
    eye = jnp.eye(RANK, dtype=gram.dtype)
    pick = jnp.concatenate([eye] * (cols // RANK), axis=0)
    norms = jnp.sqrt(jnp.sum(pick * mm(gram, pick), axis=0))
    coords = pick / norms[None, :]
    for turn in range(ITERS):
        image = mm(gram, coords)
        lower = jnp.linalg.cholesky(mm_tn(image, mm(gram, image)))
        coords = solve_lower_t(lower, image)
    weights = mm(gram, coords)
    lower = jnp.linalg.cholesky(mm_tn(weights, weights))
    return mm(coords, lower)


def shards(acts, grads, sketch_index, sketch_values):
    local_width = acts.shape[2]
    blocks = local_width // 128
    width = sketch_values.shape[4]
    tensor_pos = lax.axis_index("tensor")
    tensor_count = lax.axis_size("tensor")
    dp_pos = lax.axis_index("dp")
    dp_count = lax.axis_size("dp")
    span = jnp.arange(blocks, dtype=jnp.int32) + tensor_pos * blocks
    onehot = (sketch_index[0][:, :, None] == span[None, None, :]).astype(jnp.bfloat16)
    local = jnp.einsum(
        "sij,sicd->sjcd", onehot, sketch_values[0], preferred_element_type=jnp.float32
    )
    local = local.astype(jnp.bfloat16).reshape(2, local_width, width)
    left_part = jnp.dot(acts[0], local[0], preferred_element_type=jnp.float32)
    right_part = jnp.dot(grads[0], local[1], preferred_element_type=jnp.float32)
    both = group_sum(jnp.concatenate([left_part, right_part], axis=1), "tensor")
    both = group_gather(both, "dp")
    left_all = both[:, :width].reshape(-1, TOK_EX, width)
    right_all = both[:, width:].reshape(-1, TOK_EX, width)
    outer = jnp.sum(left_all[:, :, :, None] * right_all[:, :, None, :], axis=1)
    joined_t = outer.reshape(outer.shape[0], -1)
    gram = scatter_gather_sum(mm(joined_t, joined_t.T), "pipe")
    coords = merged_coords(gram)
    part_rows = joined_t.shape[1] // tensor_count
    rows = lax.dynamic_slice_in_dim(joined_t, tensor_pos * part_rows, part_rows, 1)
    own_columns = coords.shape[1] // dp_count
    coords = lax.dynamic_slice_in_dim(coords, dp_pos * own_columns, own_columns, 1)
    return mm_tn(rows, coords)


def solution(mesh):
    placed = (
        P("pipe", "dp", "tensor"),
        P("pipe", "dp", "tensor"),
        P("pipe", None, None),
        P("pipe", None, None, None, None),
    )
    return jax.shard_map(
        shards, mesh=mesh, in_specs=placed, out_specs=P(("pipe", "tensor"), "dp"), check_vma=False
    )
```

```python
import jax
import jax.numpy as jnp
from jax import lax
from jax.sharding import PartitionSpec as P

RANK = 256
ITERS = 2
TOK_EX = 4


def mm(a, b):
    return jnp.matmul(a, b, precision=lax.Precision.HIGHEST)


def mm_tn(a, b):
    return lax.dot_general(a, b, (((0,), (0,)), ((), ())), precision=lax.Precision.HIGHEST)


def exchange(block, axis, bit):
    count = lax.axis_size(axis)
    return lax.ppermute(block, axis, [(i, i ^ (1 << bit)) for i in range(count)])


def butterfly_sum(block, axis):
    for bit in range(lax.axis_size(axis).bit_length() - 1):
        block = block + exchange(block, axis, bit)
    return block


def halving_doubling_sum(block, axis):
    position = lax.axis_index(axis)
    bits = lax.axis_size(axis).bit_length() - 1
    for bit in range(bits):
        half = block.shape[0] // 2
        upper = jnp.right_shift(position, bit) % 2
        keep = lax.dynamic_slice_in_dim(block, upper * half, half, 0)
        give = lax.dynamic_slice_in_dim(block, (1 - upper) * half, half, 0)
        block = keep + exchange(give, axis, bit)
    return doubling_gather(block, axis, reversed(range(bits)))


def doubling_gather(block, axis, bits):
    position = lax.axis_index(axis)
    for bit in bits:
        upper = jnp.right_shift(position, bit) % 2 == 1
        other = exchange(block, axis, bit)
        block = jnp.where(
            upper, jnp.concatenate([other, block], 0), jnp.concatenate([block, other], 0)
        )
    return block


def solve_lower_t(lower, block):
    return lax.linalg.triangular_solve(lower, block, left_side=False, lower=True, transpose_a=True)


def merged_coords(gram):
    cols = gram.shape[0]
    eye = jnp.eye(RANK, dtype=gram.dtype)
    pick = jnp.concatenate([eye] * (cols // RANK), axis=0)
    norms = jnp.sqrt(jnp.sum(pick * mm(gram, pick), axis=0))
    image = mm(gram, pick / norms[None, :])
    for turn in range(ITERS):
        moved = mm(gram, image)
        lower = jnp.linalg.cholesky(mm_tn(image, moved))
        if turn + 1 < ITERS:
            image = solve_lower_t(lower, moved)
        else:
            both = solve_lower_t(lower, jnp.concatenate([image, moved], axis=0))
            coords, weights = both[:cols], both[cols:]
    lower = jnp.linalg.cholesky(mm_tn(weights, weights))
    return mm(coords, lower)


def shards(acts, grads, sketch_index, sketch_values):
    local_width = acts.shape[2]
    blocks = local_width // 128
    width = sketch_values.shape[4]
    tensor_pos = lax.axis_index("tensor")
    tensor_count = lax.axis_size("tensor")
    dp_pos = lax.axis_index("dp")
    dp_count = lax.axis_size("dp")
    span = jnp.arange(blocks, dtype=jnp.int32) + tensor_pos * blocks
    onehot = (sketch_index[0][:, :, None] == span[None, None, :]).astype(jnp.bfloat16)
    local = jnp.einsum(
        "sij,sicd->sjcd", onehot, sketch_values[0], preferred_element_type=jnp.float32
    )
    local = local.astype(jnp.bfloat16).reshape(2, local_width, width)
    left_part = jnp.dot(acts[0], local[0], preferred_element_type=jnp.float32)
    right_part = jnp.dot(grads[0], local[1], preferred_element_type=jnp.float32)
    both = butterfly_sum(jnp.concatenate([left_part, right_part], axis=1), "tensor")
    dp_bits = dp_count.bit_length() - 1
    both = doubling_gather(both, "dp", range(dp_bits))
    left_all = both[:, :width].reshape(-1, TOK_EX, width)
    right_all = both[:, width:].reshape(-1, TOK_EX, width)
    outer = jnp.sum(left_all[:, :, :, None] * right_all[:, :, None, :], axis=1)
    joined_t = outer.reshape(outer.shape[0], -1)
    gram = halving_doubling_sum(mm(joined_t, joined_t.T), "pipe")
    coords = merged_coords(gram)
    part_rows = joined_t.shape[1] // tensor_count
    rows = lax.dynamic_slice_in_dim(joined_t, tensor_pos * part_rows, part_rows, 1)
    own_columns = coords.shape[1] // dp_count
    coords = lax.dynamic_slice_in_dim(coords, dp_pos * own_columns, own_columns, 1)
    return mm_tn(rows, coords)


def solution(mesh):
    placed = (
        P("pipe", "dp", "tensor"),
        P("pipe", "dp", "tensor"),
        P("pipe", None, None),
        P("pipe", None, None, None, None),
    )
    return jax.shard_map(
        shards, mesh=mesh, in_specs=placed, out_specs=P(("pipe", "tensor"), "dp"), check_vma=False
    )
```

```python
import jax
import jax.numpy as jnp
from jax import lax
from jax.sharding import PartitionSpec as P

RANK = 256
ITERS = 2
TOK_EX = 4


def mm(a, b):
    return jnp.matmul(a, b, precision=lax.Precision.HIGHEST)


def mm_high(a, b):
    return jnp.matmul(a, b, precision=lax.Precision.HIGH)


def mm_tn_high(a, b):
    return lax.dot_general(a, b, (((0,), (0,)), ((), ())), precision=lax.Precision.HIGH)


def mm_tn(a, b):
    return lax.dot_general(a, b, (((0,), (0,)), ((), ())), precision=lax.Precision.HIGHEST)


def exchange(block, axis, bit):
    count = lax.axis_size(axis)
    return lax.ppermute(block, axis, [(i, i ^ (1 << bit)) for i in range(count)])


def butterfly_sum(block, axis):
    for bit in range(lax.axis_size(axis).bit_length() - 1):
        block = block + exchange(block, axis, bit)
    return block


def halving_doubling_sum(block, axis):
    position = lax.axis_index(axis)
    bits = lax.axis_size(axis).bit_length() - 1
    for bit in range(bits):
        half = block.shape[0] // 2
        upper = jnp.right_shift(position, bit) % 2 == 1
        keep = jnp.where(upper, block[half:], block[:half])
        give = jnp.where(upper, block[:half], block[half:])
        block = keep + exchange(give, axis, bit)
    return doubling_gather(block, axis, reversed(range(bits)))


def doubling_gather(block, axis, bits):
    position = lax.axis_index(axis)
    for bit in bits:
        upper = jnp.right_shift(position, bit) % 2 == 1
        other = exchange(block, axis, bit)
        block = jnp.where(
            upper, jnp.concatenate([other, block], 0), jnp.concatenate([block, other], 0)
        )
    return block


def solve_lower_t(lower, block):
    return lax.linalg.triangular_solve(lower, block, left_side=False, lower=True, transpose_a=True)


def merged_coords(gram):
    cols = gram.shape[0]
    eye = jnp.eye(RANK, dtype=gram.dtype)
    pick = jnp.concatenate([eye] * (cols // RANK), axis=0)
    norms = jnp.sqrt(jnp.sum(pick * mm_high(gram, pick), axis=0))
    coords = pick / norms[None, :]
    for turn in range(ITERS):
        image = mm_high(gram, coords)
        lower = jnp.linalg.cholesky(mm_tn_high(image, mm_high(gram, image)))
        coords = solve_lower_t(lower, image)
    weights = mm_high(gram, coords)
    lower = jnp.linalg.cholesky(mm_tn_high(weights, weights))
    return mm(coords, lower)


def shards(acts, grads, sketch_index, sketch_values):
    local_width = acts.shape[2]
    blocks = local_width // 128
    width = sketch_values.shape[4]
    tensor_pos = lax.axis_index("tensor")
    tensor_count = lax.axis_size("tensor")
    dp_pos = lax.axis_index("dp")
    dp_count = lax.axis_size("dp")
    span = jnp.arange(blocks, dtype=jnp.int32) + tensor_pos * blocks
    onehot = (sketch_index[0][:, :, None] == span[None, None, :]).astype(jnp.bfloat16)
    local = jnp.einsum(
        "sij,sicd->sjcd", onehot, sketch_values[0], preferred_element_type=jnp.float32
    )
    local = local.astype(jnp.bfloat16).reshape(2, local_width, width)
    left_part = jnp.dot(acts[0], local[0], preferred_element_type=jnp.float32)
    right_part = jnp.dot(grads[0], local[1], preferred_element_type=jnp.float32)
    both = butterfly_sum(jnp.concatenate([left_part, right_part], axis=1), "tensor")
    dp_bits = dp_count.bit_length() - 1
    both = doubling_gather(both, "dp", range(dp_bits))
    left_all = both[:, :width].reshape(-1, TOK_EX, width)
    right_all = both[:, width:].reshape(-1, TOK_EX, width)
    outer = jnp.sum(left_all[:, :, :, None] * right_all[:, :, None, :], axis=1)
    joined_t = outer.reshape(outer.shape[0], -1)
    gram = halving_doubling_sum(mm(joined_t, joined_t.T), "pipe")
    coords = merged_coords(gram)
    part_rows = joined_t.shape[1] // tensor_count
    rows = lax.dynamic_slice_in_dim(joined_t, tensor_pos * part_rows, part_rows, 1)
    own_columns = coords.shape[1] // dp_count
    coords = lax.dynamic_slice_in_dim(coords, dp_pos * own_columns, own_columns, 1)
    return mm_tn(rows, coords)


def solution(mesh):
    placed = (
        P("pipe", "dp", "tensor"),
        P("pipe", "dp", "tensor"),
        P("pipe", None, None),
        P("pipe", None, None, None, None),
    )
    return jax.shard_map(
        shards, mesh=mesh, in_specs=placed, out_specs=P(("pipe", "tensor"), "dp"), check_vma=False
    )
```

```python
import jax
import jax.numpy as jnp
from jax import lax
from jax.sharding import PartitionSpec as P

RANK = 256
ITERS = 2
TOK_EX = 4


def mm(a, b):
    return jnp.matmul(a, b, precision=lax.Precision.HIGHEST)


def mm_high(a, b):
    return jnp.matmul(a, b, precision=lax.Precision.HIGH)


def mm_tn_high(a, b):
    return lax.dot_general(a, b, (((0,), (0,)), ((), ())), precision=lax.Precision.HIGH)


def mm_tn(a, b):
    return lax.dot_general(a, b, (((0,), (0,)), ((), ())), precision=lax.Precision.HIGHEST)


def exchange(block, axis, bit):
    count = lax.axis_size(axis)
    return lax.ppermute(block, axis, [(i, i ^ (1 << bit)) for i in range(count)])


def butterfly_sum(block, axis):
    for bit in range(lax.axis_size(axis).bit_length() - 1):
        block = block + exchange(block, axis, bit)
    return block


def halving_doubling_sum(block, axis):
    position = lax.axis_index(axis)
    bits = lax.axis_size(axis).bit_length() - 1
    for bit in range(bits):
        half = block.shape[0] // 2
        upper = jnp.right_shift(position, bit) % 2 == 1
        keep = jnp.where(upper, block[half:], block[:half])
        give = jnp.where(upper, block[:half], block[half:])
        block = keep + exchange(give, axis, bit)
    return doubling_gather(block, axis, reversed(range(bits)))


def doubling_gather(block, axis, bits):
    position = lax.axis_index(axis)
    for bit in bits:
        upper = jnp.right_shift(position, bit) % 2 == 1
        other = exchange(block, axis, bit)
        block = jnp.where(
            upper, jnp.concatenate([other, block], 0), jnp.concatenate([block, other], 0)
        )
    return block


def solve_lower_t(lower, block):
    return lax.linalg.triangular_solve(lower, block, left_side=False, lower=True, transpose_a=True)


def cholesky_scaled(gram):
    scale = jnp.exp2(jnp.round(-0.5 * jnp.log2(jnp.diagonal(gram))))
    lower = jnp.linalg.cholesky(gram * scale[:, None] * scale[None, :])
    return lower / scale[:, None]


def merged_coords(gram):
    cols = gram.shape[0]
    eye = jnp.eye(RANK, dtype=gram.dtype)
    pick = jnp.concatenate([eye] * (cols // RANK), axis=0)
    norms = jnp.sqrt(jnp.sum(pick * mm_high(gram, pick), axis=0))
    coords = pick / norms[None, :]
    for turn in range(ITERS):
        image = mm_high(gram, coords)
        lower = cholesky_scaled(mm_tn_high(image, mm_high(gram, image)))
        coords = solve_lower_t(lower, image)
    weights = mm_high(gram, coords)
    lower = cholesky_scaled(mm_tn_high(weights, weights))
    return mm(coords, lower)


def shards(acts, grads, sketch_index, sketch_values):
    local_width = acts.shape[2]
    blocks = local_width // 128
    width = sketch_values.shape[4]
    tensor_pos = lax.axis_index("tensor")
    tensor_count = lax.axis_size("tensor")
    dp_pos = lax.axis_index("dp")
    dp_count = lax.axis_size("dp")
    span = jnp.arange(blocks, dtype=jnp.int32) + tensor_pos * blocks
    onehot = (sketch_index[0][:, :, None] == span[None, None, :]).astype(jnp.bfloat16)
    local = jnp.einsum(
        "sij,sicd->sjcd", onehot, sketch_values[0], preferred_element_type=jnp.float32
    )
    local = local.astype(jnp.bfloat16).reshape(2, local_width, width)
    left_part = jnp.dot(acts[0], local[0], preferred_element_type=jnp.float32)
    right_part = jnp.dot(grads[0], local[1], preferred_element_type=jnp.float32)
    both = butterfly_sum(jnp.concatenate([left_part, right_part], axis=1), "tensor")
    dp_bits = dp_count.bit_length() - 1
    both = doubling_gather(both, "dp", range(dp_bits))
    left_all = both[:, :width].reshape(-1, TOK_EX, width)
    right_all = both[:, width:].reshape(-1, TOK_EX, width)
    outer = jnp.sum(left_all[:, :, :, None] * right_all[:, :, None, :], axis=1)
    joined_t = outer.reshape(outer.shape[0], -1)
    gram = halving_doubling_sum(mm(joined_t, joined_t.T), "pipe")
    coords = merged_coords(gram)
    part_rows = joined_t.shape[1] // tensor_count
    rows = lax.dynamic_slice_in_dim(joined_t, tensor_pos * part_rows, part_rows, 1)
    own_columns = coords.shape[1] // dp_count
    coords = lax.dynamic_slice_in_dim(coords, dp_pos * own_columns, own_columns, 1)
    return mm_tn(rows, coords)


def solution(mesh):
    placed = (
        P("pipe", "dp", "tensor"),
        P("pipe", "dp", "tensor"),
        P("pipe", None, None),
        P("pipe", None, None, None, None),
    )
    return jax.shard_map(
        shards, mesh=mesh, in_specs=placed, out_specs=P(("pipe", "tensor"), "dp"), check_vma=False
    )
```

```python
import jax
import jax.numpy as jnp
from jax import lax
from jax.sharding import PartitionSpec as P

RANK = 256
ITERS = 2
TOK_EX = 4


def mm(a, b):
    return jnp.matmul(a, b, precision=lax.Precision.HIGHEST)


def mm_high(a, b):
    return jnp.matmul(a, b, precision=lax.Precision.HIGH)


def mm_tn_high(a, b):
    return lax.dot_general(a, b, (((0,), (0,)), ((), ())), precision=lax.Precision.HIGH)


def mm_tn(a, b):
    return lax.dot_general(a, b, (((0,), (0,)), ((), ())), precision=lax.Precision.HIGHEST)


def exchange(block, axis, bit):
    count = lax.axis_size(axis)
    return lax.ppermute(block, axis, [(i, i ^ (1 << bit)) for i in range(count)])


def butterfly_sum(block, axis):
    for bit in range(lax.axis_size(axis).bit_length() - 1):
        block = block + exchange(block, axis, bit)
    return block


def halving_doubling_sum(block, axis):
    position = lax.axis_index(axis)
    bits = lax.axis_size(axis).bit_length() - 1
    for bit in range(bits):
        half = block.shape[0] // 2
        upper = jnp.right_shift(position, bit) % 2 == 1
        keep = jnp.where(upper, block[half:], block[:half])
        give = jnp.where(upper, block[:half], block[half:])
        block = keep + exchange(give, axis, bit)
    return doubling_gather(block, axis, reversed(range(bits)))


def doubling_gather(block, axis, bits):
    position = lax.axis_index(axis)
    for bit in bits:
        upper = jnp.right_shift(position, bit) % 2 == 1
        other = exchange(block, axis, bit)
        block = jnp.where(
            upper, jnp.concatenate([other, block], 0), jnp.concatenate([block, other], 0)
        )
    return block


def solve_lower_t(lower, block):
    return lax.linalg.triangular_solve(lower, block, left_side=False, lower=True, transpose_a=True)


def cholesky_scaled(gram):
    scale = jnp.exp2(jnp.round(-0.5 * jnp.log2(jnp.diagonal(gram))))
    lower = jnp.linalg.cholesky(gram * scale[:, None] * scale[None, :])
    return lower / scale[:, None]


def merged_coords(gram):
    cols = gram.shape[0]
    eye = jnp.eye(RANK, dtype=gram.dtype)
    pick = jnp.concatenate([eye] * (cols // RANK), axis=0)
    norms = jnp.sqrt(jnp.sum(pick * mm_high(gram, pick), axis=0))
    coords = pick / norms[None, :]
    for turn in range(ITERS):
        image = mm_high(gram, coords)
        square = mm_tn_high(image, mm_high(gram, image))
        lower = cholesky_scaled(square) if turn == 0 else jnp.linalg.cholesky(square)
        coords = solve_lower_t(lower, image)
    weights = mm_high(gram, coords)
    lower = jnp.linalg.cholesky(mm_tn_high(weights, weights))
    return mm(coords, lower)


def shards(acts, grads, sketch_index, sketch_values):
    local_width = acts.shape[2]
    blocks = local_width // 128
    width = sketch_values.shape[4]
    tensor_pos = lax.axis_index("tensor")
    tensor_count = lax.axis_size("tensor")
    dp_pos = lax.axis_index("dp")
    dp_count = lax.axis_size("dp")
    span = jnp.arange(blocks, dtype=jnp.int32) + tensor_pos * blocks
    onehot = (sketch_index[0][:, :, None] == span[None, None, :]).astype(jnp.bfloat16)
    local = jnp.einsum(
        "sij,sicd->sjcd", onehot, sketch_values[0], preferred_element_type=jnp.float32
    )
    local = local.astype(jnp.bfloat16).reshape(2, local_width, width)
    left_part = jnp.dot(acts[0], local[0], preferred_element_type=jnp.float32)
    right_part = jnp.dot(grads[0], local[1], preferred_element_type=jnp.float32)
    both = butterfly_sum(jnp.concatenate([left_part, right_part], axis=1), "tensor")
    dp_bits = dp_count.bit_length() - 1
    both = doubling_gather(both, "dp", range(dp_bits))
    left_all = both[:, :width].reshape(-1, TOK_EX, width)
    right_all = both[:, width:].reshape(-1, TOK_EX, width)
    outer = jnp.sum(left_all[:, :, :, None] * right_all[:, :, None, :], axis=1)
    joined_t = outer.reshape(outer.shape[0], -1)
    gram = halving_doubling_sum(mm(joined_t, joined_t.T), "pipe")
    coords = merged_coords(gram)
    part_rows = joined_t.shape[1] // tensor_count
    rows = lax.dynamic_slice_in_dim(joined_t, tensor_pos * part_rows, part_rows, 1)
    own_columns = coords.shape[1] // dp_count
    coords = lax.dynamic_slice_in_dim(coords, dp_pos * own_columns, own_columns, 1)
    return mm_tn(rows, coords)


def solution(mesh):
    placed = (
        P("pipe", "dp", "tensor"),
        P("pipe", "dp", "tensor"),
        P("pipe", None, None),
        P("pipe", None, None, None, None),
    )
    return jax.shard_map(
        shards, mesh=mesh, in_specs=placed, out_specs=P(("pipe", "tensor"), "dp"), check_vma=False
    )
```

```python
import jax
import jax.numpy as jnp
from jax import lax
from jax.sharding import PartitionSpec as P

RANK = 256
ITERS = 2
TOK_EX = 4


def mm(a, b):
    return jnp.matmul(a, b, precision=lax.Precision.HIGHEST)


def mm_high(a, b):
    return jnp.matmul(a, b, precision=lax.Precision.HIGH)


def mm_tn_high(a, b):
    return lax.dot_general(a, b, (((0,), (0,)), ((), ())), precision=lax.Precision.HIGH)


def mm_tn(a, b):
    return lax.dot_general(a, b, (((0,), (0,)), ((), ())), precision=lax.Precision.HIGHEST)


def exchange(block, axis, bit):
    count = lax.axis_size(axis)
    return lax.ppermute(block, axis, [(i, i ^ (1 << bit)) for i in range(count)])


def butterfly_sum(block, axis):
    for bit in range(lax.axis_size(axis).bit_length() - 1):
        block = block + exchange(block, axis, bit)
    return block


def halving_doubling_sum(block, axis):
    position = lax.axis_index(axis)
    bits = lax.axis_size(axis).bit_length() - 1
    for bit in range(bits):
        half = block.shape[0] // 2
        upper = jnp.right_shift(position, bit) % 2 == 1
        keep = jnp.where(upper, block[half:], block[:half])
        give = jnp.where(upper, block[:half], block[half:])
        block = keep + exchange(give, axis, bit)
    return doubling_gather(block, axis, reversed(range(bits)))


def doubling_gather(block, axis, bits):
    position = lax.axis_index(axis)
    for bit in bits:
        upper = jnp.right_shift(position, bit) % 2 == 1
        other = exchange(block, axis, bit)
        block = jnp.where(
            upper, jnp.concatenate([other, block], 0), jnp.concatenate([block, other], 0)
        )
    return block


def pack_lower(gram, size):
    count = gram.shape[0] // size
    return jnp.concatenate(
        [gram[i * size:(i + 1) * size, j * size:(j + 1) * size] for i in range(count) for j in range(i + 1)],
        axis=0,
    )


def unpack_lower(packed, count, size):
    blocks = {}
    for i in range(count):
        for j in range(i + 1):
            at = len(blocks)
            blocks[(i, j)] = packed[at * size:(at + 1) * size]
    return jnp.concatenate(
        [
            jnp.concatenate(
                [blocks[(i, j)] if j <= i else blocks[(j, i)].T for j in range(count)], axis=1
            )
            for i in range(count)
        ],
        axis=0,
    )


def solve_lower_t(lower, block):
    return lax.linalg.triangular_solve(lower, block, left_side=False, lower=True, transpose_a=True)


def cholesky_scaled(gram):
    scale = jnp.exp2(jnp.round(-0.5 * jnp.log2(jnp.diagonal(gram))))
    lower = jnp.linalg.cholesky(gram * scale[:, None] * scale[None, :])
    return lower / scale[:, None]


def merged_coords(gram):
    cols = gram.shape[0]
    eye = jnp.eye(RANK, dtype=gram.dtype)
    pick = jnp.concatenate([eye] * (cols // RANK), axis=0)
    norms = jnp.sqrt(jnp.sum(pick * mm_high(gram, pick), axis=0))
    coords = pick / norms[None, :]
    for turn in range(ITERS):
        image = mm_high(gram, coords)
        square = mm_tn_high(image, mm_high(gram, image))
        lower = cholesky_scaled(square) if turn == 0 else jnp.linalg.cholesky(square)
        coords = solve_lower_t(lower, image)
    weights = mm_high(gram, coords)
    lower = jnp.linalg.cholesky(mm_tn_high(weights, weights))
    return mm(coords, lower)


def shards(acts, grads, sketch_index, sketch_values):
    local_width = acts.shape[2]
    blocks = local_width // 128
    width = sketch_values.shape[4]
    tensor_pos = lax.axis_index("tensor")
    tensor_count = lax.axis_size("tensor")
    dp_pos = lax.axis_index("dp")
    dp_count = lax.axis_size("dp")
    span = jnp.arange(blocks, dtype=jnp.int32) + tensor_pos * blocks
    onehot = (sketch_index[0][:, :, None] == span[None, None, :]).astype(jnp.bfloat16)
    local = jnp.einsum(
        "sij,sicd->sjcd", onehot, sketch_values[0], preferred_element_type=jnp.float32
    )
    local = local.astype(jnp.bfloat16).reshape(2, local_width, width)
    left_part = jnp.dot(acts[0], local[0], preferred_element_type=jnp.float32)
    right_part = jnp.dot(grads[0], local[1], preferred_element_type=jnp.float32)
    both = butterfly_sum(jnp.concatenate([left_part, right_part], axis=1), "tensor")
    dp_bits = dp_count.bit_length() - 1
    both = doubling_gather(both, "dp", range(dp_bits))
    left_all = both[:, :width].reshape(-1, TOK_EX, width)
    right_all = both[:, width:].reshape(-1, TOK_EX, width)
    outer = jnp.sum(left_all[:, :, :, None] * right_all[:, :, None, :], axis=1)
    joined_t = outer.reshape(outer.shape[0], -1)
    size = 128
    count = joined_t.shape[0] // size
    packed = halving_doubling_sum(pack_lower(mm(joined_t, joined_t.T), size), "pipe")
    gram = unpack_lower(packed, count, size)
    coords = merged_coords(gram)
    part_rows = joined_t.shape[1] // tensor_count
    rows = lax.dynamic_slice_in_dim(joined_t, tensor_pos * part_rows, part_rows, 1)
    own_columns = coords.shape[1] // dp_count
    coords = lax.dynamic_slice_in_dim(coords, dp_pos * own_columns, own_columns, 1)
    return mm_tn(rows, coords)


def solution(mesh):
    placed = (
        P("pipe", "dp", "tensor"),
        P("pipe", "dp", "tensor"),
        P("pipe", None, None),
        P("pipe", None, None, None, None),
    )
    return jax.shard_map(
        shards, mesh=mesh, in_specs=placed, out_specs=P(("pipe", "tensor"), "dp"), check_vma=False
    )
```

```python
import jax
import jax.numpy as jnp
from jax import lax
from jax.sharding import PartitionSpec as P

RANK = 256
ITERS = 2
TOK_EX = 4


def mm(a, b):
    return jnp.matmul(a, b, precision=lax.Precision.HIGHEST)


def mm_high(a, b):
    return jnp.matmul(a, b, precision=lax.Precision.HIGH)


def mm_tn_high(a, b):
    return lax.dot_general(a, b, (((0,), (0,)), ((), ())), precision=lax.Precision.HIGH)


def mm_tn(a, b):
    return lax.dot_general(a, b, (((0,), (0,)), ((), ())), precision=lax.Precision.HIGHEST)


def exchange(block, axis, bit):
    count = lax.axis_size(axis)
    return lax.ppermute(block, axis, [(i, i ^ (1 << bit)) for i in range(count)])


def butterfly_sum(block, axis):
    for bit in range(lax.axis_size(axis).bit_length() - 1):
        block = block + exchange(block, axis, bit)
    return block


def halving_doubling_sum(block, axis):
    position = lax.axis_index(axis)
    bits = lax.axis_size(axis).bit_length() - 1
    for bit in range(bits):
        half = block.shape[0] // 2
        upper = jnp.right_shift(position, bit) % 2 == 1
        keep = jnp.where(upper, block[half:], block[:half])
        give = jnp.where(upper, block[:half], block[half:])
        block = keep + exchange(give, axis, bit)
    return doubling_gather(block, axis, reversed(range(bits)))


def doubling_gather(block, axis, bits):
    position = lax.axis_index(axis)
    for bit in bits:
        upper = jnp.right_shift(position, bit) % 2 == 1
        other = exchange(block, axis, bit)
        block = jnp.where(
            upper, jnp.concatenate([other, block], 0), jnp.concatenate([block, other], 0)
        )
    return block


def solve_lower_t(lower, block):
    return lax.linalg.triangular_solve(lower, block, left_side=False, lower=True, transpose_a=True)


def cholesky_scaled(gram):
    scale = jnp.exp2(jnp.round(-0.5 * jnp.log2(jnp.diagonal(gram))))
    lower = jnp.linalg.cholesky(gram * scale[:, None] * scale[None, :])
    return lower / scale[:, None]


def orth_coords(square, image, scaled):
    if scaled:
        scale = jnp.exp2(jnp.round(-0.5 * jnp.log2(jnp.diagonal(square))))
        square = square * scale[:, None] * scale[None, :]
        image = image * scale[None, :]
    half = square.shape[0] // 2
    lower11 = jnp.linalg.cholesky(square[:half, :half])
    solved = solve_lower_t(lower11, jnp.concatenate([square[half:, :half], image[:, :half]], axis=0))
    lower21, first = solved[:half], solved[half:]
    lower22 = jnp.linalg.cholesky(square[half:, half:] - mm(lower21, lower21.T))
    second = solve_lower_t(lower22, image[:, half:] - mm(first, lower21.T))
    return jnp.concatenate([first, second], axis=1)


def merged_coords(gram):
    cols = gram.shape[0]
    eye = jnp.eye(RANK, dtype=gram.dtype)
    pick = jnp.concatenate([eye] * (cols // RANK), axis=0)
    norms = jnp.sqrt(jnp.sum(pick * mm_high(gram, pick), axis=0))
    coords = pick / norms[None, :]
    for turn in range(ITERS):
        image = mm_high(gram, coords)
        square = mm_tn_high(image, mm_high(gram, image))
        coords = orth_coords(square, image, turn == 0)
    weights = mm_high(gram, coords)
    lower = jnp.linalg.cholesky(mm_tn_high(weights, weights))
    return mm(coords, lower)


def shards(acts, grads, sketch_index, sketch_values):
    local_width = acts.shape[2]
    blocks = local_width // 128
    width = sketch_values.shape[4]
    tensor_pos = lax.axis_index("tensor")
    tensor_count = lax.axis_size("tensor")
    dp_pos = lax.axis_index("dp")
    dp_count = lax.axis_size("dp")
    span = jnp.arange(blocks, dtype=jnp.int32) + tensor_pos * blocks
    onehot = (sketch_index[0][:, :, None] == span[None, None, :]).astype(jnp.bfloat16)
    local = jnp.einsum(
        "sij,sicd->sjcd", onehot, sketch_values[0], preferred_element_type=jnp.float32
    )
    local = local.astype(jnp.bfloat16).reshape(2, local_width, width)
    left_part = jnp.dot(acts[0], local[0], preferred_element_type=jnp.float32)
    right_part = jnp.dot(grads[0], local[1], preferred_element_type=jnp.float32)
    both = butterfly_sum(jnp.concatenate([left_part, right_part], axis=1), "tensor")
    dp_bits = dp_count.bit_length() - 1
    both = doubling_gather(both, "dp", range(dp_bits))
    left_all = both[:, :width].reshape(-1, TOK_EX, width)
    right_all = both[:, width:].reshape(-1, TOK_EX, width)
    outer = jnp.sum(left_all[:, :, :, None] * right_all[:, :, None, :], axis=1)
    joined_t = outer.reshape(outer.shape[0], -1)
    gram = halving_doubling_sum(mm(joined_t, joined_t.T), "pipe")
    coords = merged_coords(gram)
    part_rows = joined_t.shape[1] // tensor_count
    rows = lax.dynamic_slice_in_dim(joined_t, tensor_pos * part_rows, part_rows, 1)
    own_columns = coords.shape[1] // dp_count
    coords = lax.dynamic_slice_in_dim(coords, dp_pos * own_columns, own_columns, 1)
    return mm_tn(rows, coords)


def solution(mesh):
    placed = (
        P("pipe", "dp", "tensor"),
        P("pipe", "dp", "tensor"),
        P("pipe", None, None),
        P("pipe", None, None, None, None),
    )
    return jax.shard_map(
        shards, mesh=mesh, in_specs=placed, out_specs=P(("pipe", "tensor"), "dp"), check_vma=False
    )
```

```python
import jax
import jax.numpy as jnp
from jax import lax
from jax.sharding import PartitionSpec as P

RANK = 256
ITERS = 2
TOK_EX = 4


def mm(a, b):
    return jnp.matmul(a, b, precision=lax.Precision.HIGHEST)


def mm_high(a, b):
    return jnp.matmul(a, b, precision=lax.Precision.HIGH)


def mm_tn_high(a, b):
    return lax.dot_general(a, b, (((0,), (0,)), ((), ())), precision=lax.Precision.HIGH)


def mm_tn(a, b):
    return lax.dot_general(a, b, (((0,), (0,)), ((), ())), precision=lax.Precision.HIGHEST)


def exchange(block, axis, bit):
    count = lax.axis_size(axis)
    return lax.ppermute(block, axis, [(i, i ^ (1 << bit)) for i in range(count)])


def butterfly_sum(block, axis):
    for bit in range(lax.axis_size(axis).bit_length() - 1):
        block = block + exchange(block, axis, bit)
    return block


def halving_doubling_sum(block, axis):
    position = lax.axis_index(axis)
    bits = lax.axis_size(axis).bit_length() - 1
    for bit in range(bits):
        half = block.shape[0] // 2
        upper = jnp.right_shift(position, bit) % 2 == 1
        keep = jnp.where(upper, block[half:], block[:half])
        give = jnp.where(upper, block[:half], block[half:])
        block = keep + exchange(give, axis, bit)
    return doubling_gather(block, axis, reversed(range(bits)))


def doubling_gather(block, axis, bits):
    position = lax.axis_index(axis)
    for bit in bits:
        upper = jnp.right_shift(position, bit) % 2 == 1
        other = exchange(block, axis, bit)
        block = jnp.where(
            upper, jnp.concatenate([other, block], 0), jnp.concatenate([block, other], 0)
        )
    return block


def solve_lower_t(lower, block):
    return lax.linalg.triangular_solve(lower, block, left_side=False, lower=True, transpose_a=True)


def cholesky_scaled(gram):
    scale = jnp.exp2(jnp.round(-0.5 * jnp.log2(jnp.diagonal(gram))))
    lower = jnp.linalg.cholesky(gram * scale[:, None] * scale[None, :])
    return lower / scale[:, None]


def orth_coords(square, image, scaled):
    if scaled:
        diagonal = jnp.sum(square * jnp.eye(square.shape[0], dtype=square.dtype), axis=0)
        scale = jnp.exp2(jnp.round(-0.5 * jnp.log2(diagonal)))
        square = square * scale[:, None] * scale[None, :]
        image = image * scale[None, :]
    half = square.shape[0] // 2
    lower11 = jnp.linalg.cholesky(square[:half, :half])
    solved = solve_lower_t(lower11, jnp.concatenate([square[half:, :half], image[:, :half]], axis=0))
    lower21, first = solved[:half], solved[half:]
    lower22 = jnp.linalg.cholesky(square[half:, half:] - mm(lower21, lower21.T))
    second = solve_lower_t(lower22, image[:, half:] - mm(first, lower21.T))
    return jnp.concatenate([first, second], axis=1)


def merged_coords(gram):
    cols = gram.shape[0]
    eye = jnp.eye(RANK, dtype=gram.dtype)
    pick = jnp.concatenate([eye] * (cols // RANK), axis=0)
    norms = jnp.sqrt(jnp.sum(pick * mm_high(gram, pick), axis=0))
    coords = pick / norms[None, :]
    for turn in range(ITERS):
        image = mm_high(gram, coords)
        square = mm_tn_high(image, mm_high(gram, image))
        coords = orth_coords(square, image, turn == 0)
    weights = mm_high(gram, coords)
    lower = jnp.linalg.cholesky(mm_tn_high(weights, weights))
    return mm(coords, lower)


def shards(acts, grads, sketch_index, sketch_values):
    local_width = acts.shape[2]
    blocks = local_width // 128
    width = sketch_values.shape[4]
    tensor_pos = lax.axis_index("tensor")
    tensor_count = lax.axis_size("tensor")
    dp_pos = lax.axis_index("dp")
    dp_count = lax.axis_size("dp")
    span = jnp.arange(blocks, dtype=jnp.int32) + tensor_pos * blocks
    onehot = (sketch_index[0][:, :, None] == span[None, None, :]).astype(jnp.bfloat16)
    local = jnp.einsum(
        "sij,sicd->sjcd", onehot, sketch_values[0], preferred_element_type=jnp.float32
    )
    local = local.astype(jnp.bfloat16).reshape(2, local_width, width)
    left_part = jnp.dot(acts[0], local[0], preferred_element_type=jnp.float32)
    right_part = jnp.dot(grads[0], local[1], preferred_element_type=jnp.float32)
    both = butterfly_sum(jnp.concatenate([left_part, right_part], axis=1), "tensor")
    dp_bits = dp_count.bit_length() - 1
    both = doubling_gather(both, "dp", range(dp_bits))
    left_all = both[:, :width].reshape(-1, TOK_EX, width)
    right_all = both[:, width:].reshape(-1, TOK_EX, width)
    outer = jnp.sum(left_all[:, :, :, None] * right_all[:, :, None, :], axis=1)
    joined_t = outer.reshape(outer.shape[0], -1)
    gram = halving_doubling_sum(mm_high(joined_t, joined_t.T), "pipe")
    coords = merged_coords(gram)
    part_rows = joined_t.shape[1] // tensor_count
    rows = lax.dynamic_slice_in_dim(joined_t, tensor_pos * part_rows, part_rows, 1)
    own_columns = coords.shape[1] // dp_count
    coords = lax.dynamic_slice_in_dim(coords, dp_pos * own_columns, own_columns, 1)
    return mm_tn(rows, coords)


def solution(mesh):
    placed = (
        P("pipe", "dp", "tensor"),
        P("pipe", "dp", "tensor"),
        P("pipe", None, None),
        P("pipe", None, None, None, None),
    )
    return jax.shard_map(
        shards, mesh=mesh, in_specs=placed, out_specs=P(("pipe", "tensor"), "dp"), check_vma=False
    )
```

```python
import jax
import jax.numpy as jnp
from jax import lax
from jax.sharding import PartitionSpec as P

RANK = 256
ITERS = 2
TOK_EX = 4


def mm(a, b):
    return jnp.matmul(a, b, precision=lax.Precision.HIGHEST)


def mm_high(a, b):
    return jnp.matmul(a, b, precision=lax.Precision.HIGH)


def mm_tn_high(a, b):
    return lax.dot_general(a, b, (((0,), (0,)), ((), ())), precision=lax.Precision.HIGH)


def mm_tn(a, b):
    return lax.dot_general(a, b, (((0,), (0,)), ((), ())), precision=lax.Precision.HIGHEST)


def exchange(block, axis, bit):
    count = lax.axis_size(axis)
    return lax.ppermute(block, axis, [(i, i ^ (1 << bit)) for i in range(count)])


def butterfly_sum(block, axis):
    for bit in range(lax.axis_size(axis).bit_length() - 1):
        block = block + exchange(block, axis, bit)
    return block


def halving_doubling_sum(block, axis):
    position = lax.axis_index(axis)
    bits = lax.axis_size(axis).bit_length() - 1
    for bit in range(bits):
        half = block.shape[0] // 2
        upper = jnp.right_shift(position, bit) % 2
        keep = lax.dynamic_slice_in_dim(block, upper * half, half, 0)
        give = lax.dynamic_slice_in_dim(block, (1 - upper) * half, half, 0)
        block = keep + exchange(give, axis, bit)
    return doubling_gather(block, axis, reversed(range(bits)))


def doubling_gather(block, axis, bits):
    position = lax.axis_index(axis)
    for bit in bits:
        upper = jnp.right_shift(position, bit) % 2
        other = exchange(block, axis, bit)
        rows = block.shape[0]
        both = jnp.zeros((2 * rows,) + block.shape[1:], block.dtype)
        both = lax.dynamic_update_slice_in_dim(both, block, upper * rows, 0)
        block = lax.dynamic_update_slice_in_dim(both, other, (1 - upper) * rows, 0)
    return block


def solve_lower_t(lower, block):
    return lax.linalg.triangular_solve(lower, block, left_side=False, lower=True, transpose_a=True)


def cholesky_scaled(gram):
    scale = jnp.exp2(jnp.round(-0.5 * jnp.log2(jnp.diagonal(gram))))
    lower = jnp.linalg.cholesky(gram * scale[:, None] * scale[None, :])
    return lower / scale[:, None]


def orth_coords(square, image, scaled):
    if scaled:
        diagonal = jnp.sum(square * jnp.eye(square.shape[0], dtype=square.dtype), axis=0)
        scale = jnp.exp2(jnp.round(-0.5 * jnp.log2(diagonal)))
        square = square * scale[:, None] * scale[None, :]
        image = image * scale[None, :]
    half = square.shape[0] // 2
    lower11 = jnp.linalg.cholesky(square[:half, :half])
    solved = solve_lower_t(lower11, jnp.concatenate([square[half:, :half], image[:, :half]], axis=0))
    lower21, first = solved[:half], solved[half:]
    lower22 = jnp.linalg.cholesky(square[half:, half:] - mm(lower21, lower21.T))
    second = solve_lower_t(lower22, image[:, half:] - mm(first, lower21.T))
    return jnp.concatenate([first, second], axis=1)


def merged_coords(gram):
    cols = gram.shape[0]
    eye = jnp.eye(RANK, dtype=gram.dtype)
    pick = jnp.concatenate([eye] * (cols // RANK), axis=0)
    norms = jnp.sqrt(jnp.sum(pick * mm_high(gram, pick), axis=0))
    coords = pick / norms[None, :]
    for turn in range(ITERS):
        image = mm_high(gram, coords)
        square = mm_tn_high(image, mm_high(gram, image))
        coords = orth_coords(square, image, turn == 0)
    weights = mm_high(gram, coords)
    lower = jnp.linalg.cholesky(mm_tn_high(weights, weights))
    return mm(coords, lower)


def shards(acts, grads, sketch_index, sketch_values):
    local_width = acts.shape[2]
    blocks = local_width // 128
    width = sketch_values.shape[4]
    tensor_pos = lax.axis_index("tensor")
    tensor_count = lax.axis_size("tensor")
    dp_pos = lax.axis_index("dp")
    dp_count = lax.axis_size("dp")
    span = jnp.arange(blocks, dtype=jnp.int32) + tensor_pos * blocks
    onehot = (sketch_index[0][:, :, None] == span[None, None, :]).astype(jnp.bfloat16)
    local = jnp.einsum(
        "sij,sicd->sjcd", onehot, sketch_values[0], preferred_element_type=jnp.float32
    )
    local = local.astype(jnp.bfloat16).reshape(2, local_width, width)
    left_part = jnp.dot(acts[0], local[0], preferred_element_type=jnp.float32)
    right_part = jnp.dot(grads[0], local[1], preferred_element_type=jnp.float32)
    both = butterfly_sum(jnp.concatenate([left_part, right_part], axis=1), "tensor")
    dp_bits = dp_count.bit_length() - 1
    both = doubling_gather(both, "dp", range(dp_bits))
    left_all = both[:, :width].reshape(-1, TOK_EX, width)
    right_all = both[:, width:].reshape(-1, TOK_EX, width)
    outer = jnp.sum(left_all[:, :, :, None] * right_all[:, :, None, :], axis=1)
    joined_t = outer.reshape(outer.shape[0], -1)
    gram = halving_doubling_sum(mm_high(joined_t, joined_t.T), "pipe")
    coords = merged_coords(gram)
    part_rows = joined_t.shape[1] // tensor_count
    rows = lax.dynamic_slice_in_dim(joined_t, tensor_pos * part_rows, part_rows, 1)
    own_columns = coords.shape[1] // dp_count
    coords = lax.dynamic_slice_in_dim(coords, dp_pos * own_columns, own_columns, 1)
    return mm_tn(rows, coords)


def solution(mesh):
    placed = (
        P("pipe", "dp", "tensor"),
        P("pipe", "dp", "tensor"),
        P("pipe", None, None),
        P("pipe", None, None, None, None),
    )
    return jax.shard_map(
        shards, mesh=mesh, in_specs=placed, out_specs=P(("pipe", "tensor"), "dp"), check_vma=False
    )
```

```python
import jax
import jax.numpy as jnp
from jax import lax
from jax.sharding import PartitionSpec as P

RANK = 256
ITERS = 2
TOK_EX = 4


def mm(a, b):
    return jnp.matmul(a, b, precision=lax.Precision.HIGHEST)


def mm_high(a, b):
    return jnp.matmul(a, b, precision=lax.Precision.HIGH)


def mm_tn_high(a, b):
    return lax.dot_general(a, b, (((0,), (0,)), ((), ())), precision=lax.Precision.HIGH)


def mm_tn(a, b):
    return lax.dot_general(a, b, (((0,), (0,)), ((), ())), precision=lax.Precision.HIGHEST)


def exchange(block, axis, bit):
    count = lax.axis_size(axis)
    return lax.ppermute(block, axis, [(i, i ^ (1 << bit)) for i in range(count)])


def butterfly_sum(block, axis):
    for bit in range(lax.axis_size(axis).bit_length() - 1):
        block = block + exchange(block, axis, bit)
    return block


def halving_doubling_sum(block, axis):
    position = lax.axis_index(axis)
    bits = lax.axis_size(axis).bit_length() - 1
    for bit in range(bits):
        half = block.shape[0] // 2
        upper = jnp.right_shift(position, bit) % 2 == 1
        keep = jnp.where(upper, block[half:], block[:half])
        give = jnp.where(upper, block[:half], block[half:])
        block = keep + exchange(give, axis, bit)
    return doubling_gather(block, axis, reversed(range(bits)))


def doubling_gather(block, axis, bits):
    position = lax.axis_index(axis)
    for bit in bits:
        upper = jnp.right_shift(position, bit) % 2 == 1
        other = exchange(block, axis, bit)
        block = jnp.where(
            upper, jnp.concatenate([other, block], 0), jnp.concatenate([block, other], 0)
        )
    return block


def solve_lower_t(lower, block):
    return lax.linalg.triangular_solve(lower, block, left_side=False, lower=True, transpose_a=True)


def cholesky_scaled(gram):
    scale = jnp.exp2(jnp.round(-0.5 * jnp.log2(jnp.diagonal(gram))))
    lower = jnp.linalg.cholesky(gram * scale[:, None] * scale[None, :])
    return lower / scale[:, None]


def orth_coords(square, image, scaled):
    if scaled:
        diagonal = jnp.sum(square * jnp.eye(square.shape[0], dtype=square.dtype), axis=0)
        scale = jnp.exp2(jnp.round(-0.5 * jnp.log2(diagonal)))
        square = square * scale[:, None] * scale[None, :]
        image = image * scale[None, :]
    half = square.shape[0] // 2
    lower11 = jnp.linalg.cholesky(square[:half, :half])
    solved = solve_lower_t(lower11, jnp.concatenate([square[half:, :half], image[:, :half]], axis=0))
    lower21, first = solved[:half], solved[half:]
    lower22 = jnp.linalg.cholesky(square[half:, half:] - mm(lower21, lower21.T))
    second = solve_lower_t(lower22, image[:, half:] - mm(first, lower21.T))
    return jnp.concatenate([first, second], axis=1)


def merged_coords(gram):
    cols = gram.shape[0]
    eye = jnp.eye(RANK, dtype=gram.dtype)
    pick = jnp.concatenate([eye] * (cols // RANK), axis=0)
    norms = jnp.sqrt(jnp.sum(pick * mm_high(gram, pick), axis=0))
    coords = pick / norms[None, :]
    for turn in range(ITERS):
        image = mm_high(gram, coords)
        square = mm_tn_high(image, mm_high(gram, image))
        coords = orth_coords(square, image, False)
    weights = mm_high(gram, coords)
    lower = jnp.linalg.cholesky(mm_tn_high(weights, weights))
    return mm(coords, lower)


def shards(acts, grads, sketch_index, sketch_values):
    local_width = acts.shape[2]
    blocks = local_width // 128
    width = sketch_values.shape[4]
    tensor_pos = lax.axis_index("tensor")
    tensor_count = lax.axis_size("tensor")
    dp_pos = lax.axis_index("dp")
    dp_count = lax.axis_size("dp")
    span = jnp.arange(blocks, dtype=jnp.int32) + tensor_pos * blocks
    onehot = (sketch_index[0][:, :, None] == span[None, None, :]).astype(jnp.bfloat16)
    local = jnp.einsum(
        "sij,sicd->sjcd", onehot, sketch_values[0], preferred_element_type=jnp.float32
    )
    local = local.astype(jnp.bfloat16).reshape(2, local_width, width)
    left_part = jnp.dot(acts[0], local[0], preferred_element_type=jnp.float32)
    right_part = jnp.dot(grads[0], local[1], preferred_element_type=jnp.float32)
    both = butterfly_sum(jnp.concatenate([left_part, right_part], axis=1), "tensor")
    dp_bits = dp_count.bit_length() - 1
    both = doubling_gather(both, "dp", range(dp_bits))
    left_all = both[:, :width].reshape(-1, TOK_EX, width)
    right_all = both[:, width:].reshape(-1, TOK_EX, width)
    outer = jnp.sum(left_all[:, :, :, None] * right_all[:, :, None, :], axis=1)
    joined_t = outer.reshape(outer.shape[0], -1)
    gram = halving_doubling_sum(mm_high(joined_t, joined_t.T), "pipe")
    coords = merged_coords(gram)
    part_rows = joined_t.shape[1] // tensor_count
    rows = lax.dynamic_slice_in_dim(joined_t, tensor_pos * part_rows, part_rows, 1)
    own_columns = coords.shape[1] // dp_count
    coords = lax.dynamic_slice_in_dim(coords, dp_pos * own_columns, own_columns, 1)
    return mm_tn(rows, coords)


def solution(mesh):
    placed = (
        P("pipe", "dp", "tensor"),
        P("pipe", "dp", "tensor"),
        P("pipe", None, None),
        P("pipe", None, None, None, None),
    )
    return jax.shard_map(
        shards, mesh=mesh, in_specs=placed, out_specs=P(("pipe", "tensor"), "dp"), check_vma=False
    )
```

```python
import jax
import jax.numpy as jnp
from jax import lax
from jax.sharding import PartitionSpec as P

RANK = 256
ITERS = 2
TOK_EX = 4


def mm(a, b):
    return jnp.matmul(a, b, precision=lax.Precision.HIGHEST)


def mm_high(a, b):
    return jnp.matmul(a, b, precision=lax.Precision.HIGH)


def mm_tn_high(a, b):
    return lax.dot_general(a, b, (((0,), (0,)), ((), ())), precision=lax.Precision.HIGH)


def mm_tn(a, b):
    return lax.dot_general(a, b, (((0,), (0,)), ((), ())), precision=lax.Precision.HIGHEST)


def exchange(block, axis, bit):
    count = lax.axis_size(axis)
    return lax.ppermute(block, axis, [(i, i ^ (1 << bit)) for i in range(count)])


def butterfly_sum(block, axis):
    for bit in range(lax.axis_size(axis).bit_length() - 1):
        block = block + exchange(block, axis, bit)
    return block


def halving_doubling_sum(block, axis):
    position = lax.axis_index(axis)
    bits = lax.axis_size(axis).bit_length() - 1
    for bit in range(bits):
        half = block.shape[0] // 2
        upper = jnp.right_shift(position, bit) % 2 == 1
        keep = jnp.where(upper, block[half:], block[:half])
        give = jnp.where(upper, block[:half], block[half:])
        block = keep + exchange(give, axis, bit)
    return doubling_gather(block, axis, reversed(range(bits)))


def doubling_gather(block, axis, bits):
    position = lax.axis_index(axis)
    for bit in bits:
        upper = jnp.right_shift(position, bit) % 2 == 1
        other = exchange(block, axis, bit)
        block = jnp.where(
            upper, jnp.concatenate([other, block], 0), jnp.concatenate([block, other], 0)
        )
    return block


def solve_lower_t(lower, block):
    return lax.linalg.triangular_solve(lower, block, left_side=False, lower=True, transpose_a=True)


def cholesky_scaled(gram):
    scale = jnp.exp2(jnp.round(-0.5 * jnp.log2(jnp.diagonal(gram))))
    lower = jnp.linalg.cholesky(gram * scale[:, None] * scale[None, :])
    return lower / scale[:, None]


def orth_coords(square, image, scaled):
    if scaled:
        diagonal = jnp.sum(square * jnp.eye(square.shape[0], dtype=square.dtype), axis=0)
        scale = jnp.exp2(jnp.round(-0.5 * jnp.log2(diagonal)))
        square = square * scale[:, None] * scale[None, :]
        image = image * scale[None, :]
    half = square.shape[0] // 2
    lower11 = jnp.linalg.cholesky(square[:half, :half])
    solved = solve_lower_t(lower11, jnp.concatenate([square[half:, :half], image[:, :half]], axis=0))
    lower21, first = solved[:half], solved[half:]
    lower22 = jnp.linalg.cholesky(square[half:, half:] - mm(lower21, lower21.T))
    second = solve_lower_t(lower22, image[:, half:] - mm(first, lower21.T))
    return jnp.concatenate([first, second], axis=1)


def merged_coords(gram):
    cols = gram.shape[0]
    eye = jnp.eye(RANK, dtype=gram.dtype)
    pick = jnp.concatenate([eye] * (cols // RANK), axis=0)
    norms = jnp.sqrt(jnp.sum(pick * mm_high(gram, pick), axis=0))
    coords = pick / norms[None, :]
    for turn in range(ITERS):
        image = mm_high(gram, coords)
        square = mm_tn_high(image, mm_high(gram, image))
        coords = orth_coords(square, image, False)
    weights = mm_high(gram, coords)
    lower = jnp.linalg.cholesky(mm_tn_high(weights, weights))
    return coords, lower


def shards(acts, grads, sketch_index, sketch_values):
    local_width = acts.shape[2]
    blocks = local_width // 128
    width = sketch_values.shape[4]
    tensor_pos = lax.axis_index("tensor")
    tensor_count = lax.axis_size("tensor")
    dp_pos = lax.axis_index("dp")
    dp_count = lax.axis_size("dp")
    span = jnp.arange(blocks, dtype=jnp.int32) + tensor_pos * blocks
    onehot = (sketch_index[0][:, :, None] == span[None, None, :]).astype(jnp.bfloat16)
    local = jnp.einsum(
        "sij,sicd->sjcd", onehot, sketch_values[0], preferred_element_type=jnp.float32
    )
    local = local.astype(jnp.bfloat16).reshape(2, local_width, width)
    left_part = jnp.dot(acts[0], local[0], preferred_element_type=jnp.float32)
    right_part = jnp.dot(grads[0], local[1], preferred_element_type=jnp.float32)
    both = butterfly_sum(jnp.concatenate([left_part, right_part], axis=1), "tensor")
    dp_bits = dp_count.bit_length() - 1
    both = doubling_gather(both, "dp", range(dp_bits))
    left_all = both[:, :width].reshape(-1, TOK_EX, width)
    right_all = both[:, width:].reshape(-1, TOK_EX, width)
    outer = jnp.sum(left_all[:, :, :, None] * right_all[:, :, None, :], axis=1)
    joined_t = outer.reshape(outer.shape[0], -1)
    gram = halving_doubling_sum(mm_high(joined_t, joined_t.T), "pipe")
    coords, lower = merged_coords(gram)
    part_rows = joined_t.shape[1] // tensor_count
    rows = lax.dynamic_slice_in_dim(joined_t, tensor_pos * part_rows, part_rows, 1)
    own_columns = lower.shape[1] // dp_count
    coords = mm(coords, lax.dynamic_slice_in_dim(lower, dp_pos * own_columns, own_columns, 1))
    return mm_tn(rows, coords)


def solution(mesh):
    placed = (
        P("pipe", "dp", "tensor"),
        P("pipe", "dp", "tensor"),
        P("pipe", None, None),
        P("pipe", None, None, None, None),
    )
    return jax.shard_map(
        shards, mesh=mesh, in_specs=placed, out_specs=P(("pipe", "tensor"), "dp"), check_vma=False
    )
```
